32 devices in a mesh: dp: 16 (over z, y, x), tensor: 2 (over core).
Axes of the slice: x: 2, y: 2, z: 4, core: 2. Of those that a mesh axis runs over, the one named last changes fastest.
Arguments:
- clip_tokens: float32 [16, 640, 768], P('dp', 'tensor'), may hold values from -6 to 6
- frame_counts: int32 [16], P('dp'), may hold values from 4 to 16, as said below
- attn_qkv: float32 [768, 3, 768], P('dp', None, 'tensor'), may hold values from -0.21875 to 0.21875
- attn_out: float32 [768, 768], P('tensor', 'dp'), may hold values from -0.875 to 0.875
- mlp_in: float32 [768, 3072], P('dp', 'tensor'), may hold values from -0.21875 to 0.21875
- mlp_out: float32 [3072, 768], P('tensor', 'dp'), may hold values from -0.109375 to 0.109375
- align_proj: float32 [768, 1024], P(('dp', 'tensor')), may hold values from -0.21875 to 0.21875
- norm_gains: float32 [2, 768], P(None, ('dp', 'tensor')), may hold values from 0.5 to 1.5
- layer_biases: float32 [6, 768], P(None, ('dp', 'tensor')), may hold values from -2 to 2
- hidden_bias: float32 [3072], P(('dp', 'tensor')), may hold values from -2 to 2
- align_bias: float32 [1024], P(('dp', 'tensor')), may hold values from -2 to 2
- out_cotangent: float32 [16, 640, 768], P('dp', 'tensor'), may hold values from -6 to 6
- align_cotangent: float32 [16, 640, 1024], P('dp', 'tensor'), may hold values from -6 to 6
Outputs:
- block_out: float32 [16, 640, 768], P('dp', 'tensor')
- align_out: float32 [16, 640, 1024], P('dp', 'tensor')
- grad_tokens: float32 [16, 640, 768], P('dp', 'tensor')
- grad_qkv: float32 [768, 3, 768], P('dp', None, 'tensor')
- grad_attn_out: float32 [768, 768], P('tensor', 'dp')
- grad_mlp_in: float32 [768, 3072], P('dp', 'tensor')
- grad_mlp_out: float32 [3072, 768], P('tensor', 'dp')
- grad_align_proj: float32 [768, 1024], P(('dp', 'tensor'))
- grad_gains: float32 [2, 768], P(None, ('dp', 'tensor'))
- grad_biases: float32 [6, 768], P(None, ('dp', 'tensor'))
- grad_hidden_bias: float32 [3072], P(('dp', 'tensor'))
- grad_align_bias: float32 [1024], P(('dp', 'tensor'))
The draws below stay inside these ranges and needn't reach their ends.
Inputs may be any that keep to these rules, and one draw needn't show every extreme that they name: `frame_counts`: each clip has 4, 8 or 16 frames, and each of the three counts occurs.
All inputs are finite; a program needn't handle non-finite values.
Results may differ from the reference program's by a relative error of at most 0.0003.
Values sent between devices are 32-bit elements; how exact they have to be, the bound alone decides.
No kernel may reach another device: no remote copies, remote signals or barrier semaphores. Data moves between devices by JAX's collectives and lax.ppermute only.
A program may use at most 192 MiB of HBM per device.

```python
import jax
import jax.numpy as jnp
from jax import lax

D = 768
HEADS = 12
HEAD_DIM = 64
FF = 3072
ALIGN = 1024
ROWS = 640
FULL_TOK = 627
CLIP_DEV = 1
CLIPS = 16
N_DP = 16


def draw_frame_counts(key, part):
    levels = jax.random.randint(key, (CLIPS,), 0, 3)
    position = jnp.arange(CLIPS, dtype=jnp.int32)
    levels = jnp.where(position < 3, 2 - position, levels)
    return jnp.where(levels == 0, 4, jnp.where(levels == 1, 8, 16)).astype(jnp.int32)


def block_scale(own_key, shape, split, least, top_value):
    gain = 1.0
    for dim, shards_of in split:
        draws = jax.random.uniform(jax.random.fold_in(jax.random.fold_in(own_key, 6), dim), (shards_of,), jnp.float32, least / len(split), top_value / len(split))
        gain = gain * jnp.repeat(jnp.exp(draws), shape[dim] // shards_of).reshape((-1,) + (1,) * (len(shape) - 1 - dim))
    return gain


def noise(own_key, shape, width, reach, cuts=(), kind=jnp.bfloat16):
    values = jax.random.normal(own_key, shape, jnp.float32) * width
    if len(cuts) > 0:
        values = block_scale(own_key, shape, cuts, -0.22, 0.18) * values
    return jnp.clip(values, min=-reach, max=reach).astype(kind)


def setup_inputs(seed: int = 0) -> dict:
    key_list = jax.random.split(jax.random.key(seed), 14)
    clip_tokens = noise(key_list[0], (CLIPS, ROWS, D), 1.0, 6.0, ((0, 16), (1, 2)), jnp.float32)
    frame_counts = draw_frame_counts(jax.random.fold_in(key_list[13], 71), 0)
    attn_qkv = noise(key_list[2], (D, 3, D), D ** -0.5, 0.21875, ((0, 16), (2, 2)), jnp.float32)
    attn_out = noise(key_list[3], (D, D), (D // 16) ** -0.5, 0.875, ((0, 2), (1, 16)), jnp.float32)
    mlp_in = noise(key_list[4], (D, FF), D ** -0.5, 0.21875, ((0, 16), (1, 2)), jnp.float32)
    mlp_out = noise(key_list[5], (FF, D), FF ** -0.5, 0.109375, ((0, 2), (1, 16)), jnp.float32)
    align_proj = noise(key_list[6], (D, ALIGN), D ** -0.5, 0.21875, ((0, 32),), jnp.float32)
    norm_gains = jnp.clip(1.0 + 0.1 * jax.random.normal(key_list[7], (2, D), jnp.float32), 0.5, 1.5)
    layer_biases = noise(key_list[8], (6, D), 0.3, 2.0, ((1, 32),), jnp.float32)
    hidden_bias = noise(key_list[9], (FF,), 0.3, 2.0, ((0, 32),), jnp.float32)
    align_bias = noise(key_list[10], (ALIGN,), 0.3, 2.0, ((0, 32),), jnp.float32)
    out_cotangent = noise(key_list[11], (CLIPS, ROWS, D), 1.0, 6.0, ((0, 16), (1, 2)), jnp.float32)
    align_cotangent = noise(key_list[12], (CLIPS, ROWS, ALIGN), 1.0, 6.0, ((0, 16), (1, 2)), jnp.float32)
    return {"clip_tokens": clip_tokens, "frame_counts": frame_counts, "attn_qkv": attn_qkv, "attn_out": attn_out, "mlp_in": mlp_in, "mlp_out": mlp_out, "align_proj": align_proj, "norm_gains": norm_gains, "layer_biases": layer_biases, "hidden_bias": hidden_bias, "align_bias": align_bias, "out_cotangent": out_cotangent, "align_cotangent": align_cotangent}


@jax.custom_vjp
def low(v):
    return lax.optimization_barrier(v.astype(jnp.bfloat16)).astype(jnp.float32)

@jax.custom_vjp
def low_back(v):
    return v

def low_keep(v):
    return (low(v), None)

def low_pass(kept, grad):
    return (grad,)

def back_keep(v):
    return (v, None)

def back_low(kept, grad):
    return (low(grad),)
low.defvjp(low_keep, low_pass)
low_back.defvjp(back_keep, back_low)
HIGHEST = lax.Precision.HIGHEST
EPSILON = 1e-06
NEG_FILL = -1e+30

def layer_norm(values, gain_row, shift_row):
    row_mean = lax.optimization_barrier(jnp.mean(values, axis=-1, keepdims=True))
    centred = values - row_mean
    variance = lax.optimization_barrier(jnp.mean(centred * centred, axis=-1, keepdims=True))
    return centred * lax.rsqrt(variance + EPSILON) * gain_row + shift_row

def forward(params, tokens, counts):
    attn_qkv, attn_out, mlp_in, mlp_out, align_proj, norm_gains, layer_biases, hidden_bias, align_bias = params
    groups = tokens.shape[0]
    kept_rows = (counts * FULL_TOK + 15) // 16
    row_index = jnp.arange(ROWS, dtype=jnp.int32)
    key_valid = row_index[None, :] < kept_rows[:, None]
    row_mask = key_valid.astype(jnp.float32)[:, :, None]
    normed_one = layer_norm(tokens, norm_gains[0], layer_biases[0])
    mixed = jnp.einsum('crd,dje->crje', normed_one, attn_qkv, precision=HIGHEST)
    query_part = (mixed[:, :, 0] + layer_biases[2]).reshape(groups, ROWS, HEADS, HEAD_DIM)
    key_part = mixed[:, :, 1].reshape(groups, ROWS, HEADS, HEAD_DIM)
    value_part = (mixed[:, :, 2] + layer_biases[3]).reshape(groups, ROWS, HEADS, HEAD_DIM)

    def attend(item):
        query_one, key_one, value_one, valid_one = item
        scores = jnp.einsum('qhe,khe->hqk', query_one, key_one, precision=HIGHEST) * HEAD_DIM ** (-0.5)
        scores = jnp.where(valid_one[None, None, :], scores, NEG_FILL)
        probs = jax.nn.softmax(scores, axis=-1)
        return jnp.einsum('hqk,khe->qhe', probs, value_one, precision=HIGHEST).reshape(ROWS, D)
    heads_out = lax.map(jax.checkpoint(attend), (query_part, key_part, value_part, key_valid))
    residual = tokens + jnp.einsum('crf,fd->crd', heads_out, attn_out, precision=HIGHEST) + layer_biases[4]
    normed_two = layer_norm(residual, norm_gains[1], layer_biases[1])
    pre_act = jnp.einsum('crd,df->crf', normed_two, mlp_in, precision=HIGHEST) + hidden_bias
    activ = jax.nn.gelu(pre_act, approximate=False)
    branch = jnp.einsum('crf,fd->crd', activ, mlp_out, precision=HIGHEST) + layer_biases[5]
    block_out = row_mask * (residual + branch)
    align_out = row_mask * (jnp.einsum('crd,da->cra', block_out, align_proj, precision=HIGHEST) + align_bias)
    return (block_out, align_out)

def reference(clip_tokens, frame_counts, attn_qkv, attn_out, mlp_in, mlp_out, align_proj, norm_gains, layer_biases, hidden_bias, align_bias, out_cotangent, align_cotangent):
    params = (attn_qkv, attn_out, mlp_in, mlp_out, align_proj, norm_gains, layer_biases, hidden_bias, align_bias)

    def group_view(array):
        return array.reshape((N_DP, CLIP_DEV) + array.shape[1:])

    def step(totals, item):
        tokens, counts, out_grad, align_grad = item
        outputs, pull = jax.vjp(lambda weights, inputs: forward(weights, inputs, counts), params, tokens)
        grad_params, grad_inputs = pull((out_grad, align_grad))
        totals = jax.tree.map(lambda running, update: running + update, totals, grad_params)
        return (totals, (outputs[0], outputs[1], grad_inputs))
    start = jax.tree.map(jnp.zeros_like, params)
    totals, stacked = lax.scan(step, start, (group_view(clip_tokens), group_view(frame_counts), group_view(out_cotangent), group_view(align_cotangent)))

    def whole(array):
        return array.reshape((CLIPS,) + array.shape[2:])
    return (whole(stacked[0]), whole(stacked[1]), whole(stacked[2]), totals[0], totals[1], totals[2], totals[3], totals[4], totals[5], totals[6], totals[7], totals[8])
```

```python
import math

import jax
import jax.numpy as jnp
from jax import lax
from jax.sharding import PartitionSpec as P

HEAD_DIM = 64
FULL_TOK = 627

HIGH = lax.Precision.HIGH
HIGHEST = lax.Precision.HIGHEST
EPSILON = 1e-06
NEG_FILL = -1e30
INV_ROOT_TWO = 1.0 / math.sqrt(2.0)
INV_ROOT_TWO_PI = 1.0 / math.sqrt(2.0 * math.pi)


def matmul(form, left_side, right_side, precision=HIGH):
    return jnp.einsum(
        form, left_side, right_side, precision=precision, preferred_element_type=jnp.float32
    )


def swap(values):
    return lax.ppermute(values, "tensor", [(0, 1), (1, 0)])


def exchange(values, bit):
    n_dp = lax.axis_size("dp")
    return lax.ppermute(values, "dp", [(i, i ^ (1 << bit)) for i in range(n_dp)])


def far_bits():
    return list(range(2, (lax.axis_size("dp") - 1).bit_length()))


def gather_blocks(shard):
    far = far_bits()
    near = shard
    for bit in far[:-1]:
        near = jnp.concatenate([near, exchange(near, bit)])
    away = exchange(near, far[-1])
    near_y, near_x = exchange(near, 1), exchange(near, 0)
    near_xy = exchange(near_y, 0)
    away_x, away_y = exchange(away, 0), exchange(away, 1)
    away_xy = exchange(away_x, 1)
    return jnp.concatenate([near, away, near_y, away_y, near_x, away_x, near_xy, away_xy])


def reduce_blocks(make):
    far = far_bits()
    near_xy, away_xy = make(6), make(7)
    got_x = exchange(near_xy, 0)
    got_y = exchange(away_xy, 1)
    near_x, away_y = make(4), make(3)
    near_from_x = exchange(near_x, 0)
    away_from_y = exchange(away_y, 1)
    near_y, away_x = make(2) + got_x, make(5) + got_y
    near_from_y = exchange(near_y, 1)
    away_from_x = exchange(away_x, 0)
    away = make(1) + away_from_y + away_from_x
    total = make(0) + near_from_x + near_from_y + exchange(away, far[-1])
    for bit in reversed(far[:-1]):
        half = total.shape[0] // 2
        total = total[:half] + exchange(total[half:], bit)
    return total


def sliced(values):
    rows = values.shape[0] // 8
    return lambda i: values[i * rows : (i + 1) * rows]


def block_masks():
    n_dp = lax.axis_size("dp")
    order = far_bits() + [1, 0]
    return [sum(((j >> i) & 1) << bit for i, bit in enumerate(order)) for j in range(n_dp)]


def centre(values):
    row_mean = jnp.mean(values, axis=-1, keepdims=True)
    centred = values - row_mean
    variance = jnp.mean(centred * centred, axis=-1, keepdims=True)
    inv = lax.rsqrt(variance + EPSILON)
    return centred * inv, inv


def norm_back(xhat, inv, scaled):
    return inv * (
        scaled
        - jnp.mean(scaled, axis=-1, keepdims=True)
        - xhat * jnp.mean(scaled * xhat, axis=-1, keepdims=True)
    )


def shards(
    clip_tokens,
    frame_counts,
    attn_qkv,
    attn_out,
    mlp_in,
    mlp_out,
    align_proj,
    norm_gains,
    layer_biases,
    hidden_bias,
    align_bias,
    out_cotangent,
    align_cotangent,
):
    n_dp = lax.axis_size("dp")
    me = lax.axis_index("dp")
    rank = lax.axis_index("tensor")
    first = rank == 0
    half = clip_tokens.shape[1]
    width = clip_tokens.shape[2]
    all_rows = 2 * half
    block = width // n_dp
    head_width = attn_qkv.shape[2]
    heads = head_width // HEAD_DIM
    hidden_width = mlp_in.shape[1]
    align_width = align_proj.shape[1]
    align_half = align_width // 2
    sub = align_proj.shape[0]
    score_scale = HEAD_DIM ** (-0.5)

    qkv_all = gather_blocks(attn_qkv.reshape(block, 3 * head_width))
    small = jnp.concatenate(
        [norm_gains.reshape(-1), layer_biases.reshape(-1), hidden_bias, align_bias]
    )
    small_other = swap(small)
    small_pair = jnp.where(
        first, jnp.stack([small, small_other]), jnp.stack([small_other, small])
    ).reshape(1, -1)
    small_rel = small_pair
    for bit in far_bits() + [1, 0]:
        small_rel = jnp.concatenate([small_rel, exchange(small_rel, bit)])

    masks = jnp.array(block_masks(), dtype=jnp.int32)
    owners = me ^ masks
    hot = (jnp.arange(n_dp, dtype=jnp.int32)[:, None] == owners[None, :]).astype(jnp.float32)
    feature = jnp.arange(width, dtype=jnp.int32)
    absolute = jnp.repeat(owners, block) * block + feature % block
    permute = (feature[:, None] == absolute[None, :]).astype(jnp.float32)

    out_all = gather_blocks(attn_out.T)
    align_other = swap(align_proj)
    align_rows = jnp.where(
        first,
        jnp.concatenate([align_proj[:, :align_half], align_other[:, :align_half]]),
        jnp.concatenate([align_other[:, align_half:], align_proj[:, align_half:]]),
    )
    align_mine = gather_blocks(align_rows)
    in_all = gather_blocks(mlp_in)
    down_all = gather_blocks(mlp_out.T)

    small_abs = matmul("ab,bc->ac", hot, small_rel, HIGHEST).reshape(n_dp, 2, -1)
    gains = small_abs[:, :, : 2 * sub].reshape(n_dp, 2, 2, sub)
    gains = jnp.transpose(gains, (2, 0, 1, 3)).reshape(2, width)
    biases = small_abs[:, :, 2 * sub : 8 * sub].reshape(n_dp, 2, 6, sub)
    biases = jnp.transpose(biases, (2, 0, 1, 3)).reshape(6, width)
    hidden_at = 8 * sub
    align_at = hidden_at + hidden_bias.shape[0]
    hidden_all = small_abs[:, :, hidden_at:align_at].reshape(-1)
    align_shift = small_abs[:, :, align_at:].reshape(-1)
    vectors = matmul("ad,de->ae", jnp.concatenate([gains, biases]), permute, HIGHEST)
    gain_one, gain_two, shift_one, shift_two = vectors[0], vectors[1], vectors[2], vectors[3]
    shift_out, shift_down = vectors[6], vectors[7]
    query_shift = jnp.where(first, biases[2, :head_width], biases[2, head_width:])
    value_shift = jnp.where(first, biases[3, :head_width], biases[3, head_width:])
    hidden_shift = jnp.where(first, hidden_all[:hidden_width], hidden_all[hidden_width:])

    kept = (frame_counts[0] * FULL_TOK + 15) // 16
    position = jnp.arange(half, dtype=jnp.int32)
    index = jnp.concatenate([rank * half + position, (1 - rank) * half + position])
    valid = index < kept
    row_mask = valid[:half].astype(jnp.float32)[:, None]

    tokens = matmul("rd,de->re", clip_tokens[0], permute, HIGHEST)
    tokens = jnp.concatenate([tokens, swap(tokens)])
    cotangent = matmul("rd,de->re", out_cotangent[0], permute, HIGHEST)

    xhat_one, inv_one = centre(tokens)
    normed_one = xhat_one * gain_one + shift_one
    mixed = matmul("rd,de->re", normed_one, qkv_all)
    query = (mixed[:, :head_width] + query_shift).reshape(all_rows, heads, HEAD_DIM)
    key = mixed[:, head_width : 2 * head_width].reshape(all_rows, heads, HEAD_DIM)
    value = (mixed[:, 2 * head_width :] + value_shift).reshape(all_rows, heads, HEAD_DIM)
    scores = matmul("qhe,khe->hqk", query, key) * score_scale
    scores = jnp.where(valid[None, None, :], scores, NEG_FILL)
    maxima = jnp.max(scores, axis=2, keepdims=True)
    expon = jnp.exp(scores - maxima)
    totals = jnp.sum(expon, axis=2, keepdims=True)
    probs = expon / totals
    heads_out = matmul("hqk,khe->qhe", probs, value).reshape(all_rows, head_width)
    attn_terms = matmul("rf,df->rd", heads_out, out_all)
    attn_sum = attn_terms + jnp.concatenate([swap(attn_terms[half:]), swap(attn_terms[:half])])
    residual = tokens + attn_sum + shift_out

    align_far = swap(align_mine)
    align_all = jnp.where(
        first,
        jnp.concatenate([align_mine, align_far], axis=1),
        jnp.concatenate([align_far, align_mine], axis=1),
    )
    align_grad = row_mask * align_cotangent[0]
    own_grad = row_mask * (cotangent + matmul("ra,da->rd", align_grad, align_all))
    out_grad = jnp.concatenate([own_grad, swap(own_grad)])

    xhat_two, inv_two = centre(residual)
    normed_two = xhat_two * gain_two + shift_two
    pre_act = matmul("rd,df->rf", normed_two, in_all) + hidden_shift
    normal_cdf = 0.5 * (1.0 + lax.erf(pre_act * INV_ROOT_TWO))
    activ = pre_act * normal_cdf
    slope = normal_cdf + pre_act * (jnp.exp(-0.5 * pre_act * pre_act) * INV_ROOT_TWO_PI)
    grad_act = matmul("rd,df->rf", out_grad, down_all) * slope
    normed_terms = matmul("rf,df->rd", grad_act, in_all)
    grad_normed_two = normed_terms + jnp.concatenate(
        [swap(normed_terms[half:]), swap(normed_terms[:half])]
    )
    grad_in = matmul("rd,rf->df", normed_two, grad_act)
    grad_in_own = reduce_blocks(sliced(grad_in))
    grad_down = matmul("rd,rf->df", out_grad, activ)
    grad_down_own = reduce_blocks(sliced(grad_down))
    hidden_part = jnp.sum(grad_act, axis=0)

    mlp_terms = matmul("rf,df->rd", activ, down_all)
    mlp_local = mlp_terms[:half] + swap(mlp_terms[half:])
    block_rel = row_mask * (residual[:half] + mlp_local + shift_down)
    align_out = row_mask * (matmul("rd,da->ra", block_rel, align_all) + align_shift)
    grad_align = matmul("rd,ra->da", block_rel, align_grad)
    align_left, align_right = grad_align[:, :align_half], grad_align[:, align_half:]
    grad_align_half = jnp.where(first, align_left, align_right) + swap(
        jnp.where(first, align_right, align_left)
    )
    grad_align_pair = reduce_blocks(sliced(grad_align_half))

    grad_residual = out_grad + norm_back(xhat_two, inv_two, grad_normed_two * gain_two)
    heads_grad = matmul("rd,df->rf", grad_residual, out_all)
    grad_out = matmul("rd,rf->df", grad_residual, heads_out)
    grad_out_own = reduce_blocks(sliced(grad_out))

    grad_split = heads_grad.reshape(all_rows, heads, HEAD_DIM)
    out_split = heads_out.reshape(all_rows, heads, HEAD_DIM)
    value_grad = matmul("hqk,qhe->khe", probs, grad_split)
    probs_grad = matmul("qhe,khe->hqk", grad_split, value)
    row_dot = jnp.transpose(jnp.sum(grad_split * out_split, axis=2))[:, :, None]
    score_grad = probs * (probs_grad - row_dot) * score_scale
    query_grad = matmul("hqk,khe->qhe", score_grad, key).reshape(all_rows, head_width)
    key_grad = matmul("hqk,qhe->khe", score_grad, query).reshape(all_rows, head_width)
    mixed_grad = jnp.concatenate(
        [query_grad, key_grad, value_grad.reshape(all_rows, head_width)], axis=1
    )
    grad_qkv = matmul("rd,re->de", normed_one, mixed_grad)
    grad_qkv_own = reduce_blocks(sliced(grad_qkv))
    one_terms = matmul("re,de->rd", mixed_grad, qkv_all)
    grad_normed_one = one_terms[:half] + swap(one_terms[half:])
    xhat_own, inv_own = xhat_one[:half], inv_one[:half]
    tokens_rel = grad_residual[:half] + norm_back(xhat_own, inv_own, grad_normed_one * gain_one)
    back = matmul("rd,ed->re", jnp.concatenate([block_rel, tokens_rel]), permute, HIGHEST)
    block_out, grad_tokens = back[:half], back[half:]

    two_own = grad_normed_two[:half]
    relative = jnp.stack(
        [
            jnp.sum(grad_normed_one * xhat_own, axis=0),
            jnp.sum(two_own * xhat_two[:half], axis=0),
            jnp.sum(grad_normed_one, axis=0),
            jnp.sum(two_own, axis=0),
            jnp.sum(grad_residual[:half], axis=0),
            jnp.sum(own_grad, axis=0),
        ]
    )
    vectors = matmul("ad,ed->ae", relative, permute, HIGHEST)

    def placed_half(part):
        zero = jnp.zeros_like(part)
        return jnp.where(first, jnp.concatenate([part, zero]), jnp.concatenate([zero, part]))

    query_sum = placed_half(jnp.sum(query_grad, axis=0))
    value_sum = placed_half(jnp.sum(mixed_grad[:, 2 * head_width :], axis=0))
    rows = jnp.stack(
        [
            vectors[0],
            vectors[1],
            vectors[2],
            vectors[3],
            query_sum,
            value_sum,
            vectors[4],
            vectors[5],
        ]
    )
    rows = jnp.transpose(rows.reshape(8, n_dp, 2, sub), (1, 2, 0, 3)).reshape(n_dp, 2, 8 * sub)
    hidden_rows = placed_half(hidden_part).reshape(n_dp, 2, -1)
    align_rows_sum = jnp.sum(align_grad, axis=0).reshape(n_dp, 2, -1)
    packed = jnp.concatenate([rows, hidden_rows, align_rows_sum], axis=2)
    packed_own = jnp.where(first, packed[:, 0], packed[:, 1]) + swap(
        jnp.where(first, packed[:, 1], packed[:, 0])
    )
    reduced = matmul("ba,bc->ac", hot, packed_own, HIGHEST)
    for bit in reversed(far_bits() + [1, 0]):
        count = reduced.shape[0] // 2
        reduced = reduced[:count] + exchange(reduced[count:], bit)
    reduced = reduced[0]

    mine = jnp.where(first, grad_align_pair[:sub], grad_align_pair[sub:])
    others = swap(jnp.where(first, grad_align_pair[sub:], grad_align_pair[:sub]))
    align_own = jnp.where(
        first,
        jnp.concatenate([mine, others], axis=1),
        jnp.concatenate([others, mine], axis=1),
    )
    return (
        block_out[None],
        align_out[None],
        grad_tokens[None],
        grad_qkv_own.reshape(block, 3, head_width),
        grad_out_own.T,
        grad_in_own,
        grad_down_own.T,
        align_own,
        reduced[: 2 * sub].reshape(2, sub),
        reduced[2 * sub : 8 * sub].reshape(6, sub),
        reduced[hidden_at:align_at],
        reduced[align_at:],
    )


def solution(mesh):
    placed = (
        P("dp", "tensor", None),
        P("dp"),
        P("dp", None, "tensor"),
        P("tensor", "dp"),
        P("dp", "tensor"),
        P("tensor", "dp"),
        P(("dp", "tensor"), None),
        P(None, ("dp", "tensor")),
        P(None, ("dp", "tensor")),
        P(("dp", "tensor")),
        P(("dp", "tensor")),
        P("dp", "tensor", None),
        P("dp", "tensor", None),
    )
    return jax.shard_map(
        shards,
        mesh=mesh,
        in_specs=placed,
        out_specs=(
            P("dp", "tensor", None),
            P("dp", "tensor", None),
            P("dp", "tensor", None),
            P("dp", None, "tensor"),
            P("tensor", "dp"),
            P("dp", "tensor"),
            P("tensor", "dp"),
            P(("dp", "tensor"), None),
            P(None, ("dp", "tensor")),
            P(None, ("dp", "tensor")),
            P(("dp", "tensor")),
            P(("dp", "tensor")),
        ),
        check_vma=False,
    )
```

```python
import math

import jax
import jax.numpy as jnp
from jax import lax
from jax.sharding import PartitionSpec as P

HEAD_DIM = 64
FULL_TOK = 627

HIGH = lax.Precision.HIGH
HIGHEST = lax.Precision.HIGHEST
EPSILON = 1e-06
NEG_FILL = -1e30
INV_ROOT_TWO = 1.0 / math.sqrt(2.0)
INV_ROOT_TWO_PI = 1.0 / math.sqrt(2.0 * math.pi)


def product(left, right, left_dim, right_dim, precision=HIGH):
    return lax.dot_general(
        left,
        right,
        (((left_dim,), (right_dim,)), ((), ())),
        precision=precision,
        preferred_element_type=jnp.float32,
    )


def mm(left, right, precision=HIGH):
    return product(left, right, 1, 0, precision)


def mm_nt(left, right, precision=HIGH):
    return product(left, right, 1, 1, precision)


def mm_tn(left, right, precision=HIGH):
    return product(left, right, 0, 0, precision)


def heads_mm(form, left, right):
    return jnp.einsum(form, left, right, precision=HIGH, preferred_element_type=jnp.float32)


def swap(values):
    return lax.ppermute(values, "tensor", [(0, 1), (1, 0)])


def exchange(values, bit):
    n_dp = lax.axis_size("dp")
    return lax.ppermute(values, "dp", [(i, i ^ (1 << bit)) for i in range(n_dp)])


def after(value, *others):
    return lax.optimization_barrier((value, *others))[0]


def inner_bits():
    return list(range(3, (lax.axis_size("dp") - 1).bit_length()))


EIGHTHS = (0, 1, 2, 5, 6, 4, 7, 3)


def block_masks():
    n_dp = lax.axis_size("dp")
    inner = inner_bits()
    masks = []
    for eighth in EIGHTHS:
        outer = (eighth >> 2 & 1) | (eighth >> 1 & 1) << 1 | (eighth & 1) << 2
        for j in range(n_dp // 8):
            masks.append(outer | sum((j >> i & 1) << bit for i, bit in enumerate(inner)))
    return masks


def gather_far(shard):
    near = shard
    for bit in inner_bits():
        near = jnp.concatenate([near, exchange(near, bit)])
    return near


def gather_side(quarter):
    return exchange(quarter, 1), exchange(quarter, 0)


def gather_corner(sides):
    side_y, side_x = sides
    eighth = side_y.shape[0] // 2
    low, high = lax.optimization_barrier((side_y[:eighth], side_x[eighth:]))
    return exchange(low, 0), exchange(high, 1)


def assemble(quarter, sides, corners):
    side_y, side_x = sides
    eighth = side_y.shape[0] // 2
    return jnp.concatenate(
        [
            quarter,
            side_y[:eighth],
            side_x[eighth:],
            corners[0],
            side_x[:eighth],
            corners[1],
            side_y[eighth:],
        ]
    )


def reduce_send(upper):
    quarter = upper.shape[0] // 2
    return exchange(upper[:quarter], 0), exchange(upper[quarter:], 1)


def reduce_turn(lower, got):
    eighth = lower.shape[0] // 4
    got_x, got_y = got
    by_y = exchange(lower[2 * eighth : 3 * eighth] + got_x[:eighth], 1)
    by_x = exchange(lower[3 * eighth :] + got_y[:eighth], 0)
    return by_y, by_x


def reduce_near(lower, got, turned):
    eighth = lower.shape[0] // 4
    got_x, got_y = got
    by_y, by_x = turned
    away = exchange(lower[eighth : 2 * eighth] + got_y[eighth:] + by_x, 2)
    return lower[:eighth] + got_x[eighth:] + by_y + away


def reduce_far(total):
    for bit in reversed(inner_bits()):
        count = total.shape[0] // 2
        total = total[:count] + exchange(total[count:], bit)
    return total


def centre(values):
    row_mean = jnp.mean(values, axis=-1, keepdims=True)
    centred = values - row_mean
    variance = jnp.mean(centred * centred, axis=-1, keepdims=True)
    inv = lax.rsqrt(variance + EPSILON)
    return centred * inv, inv


def norm_back(xhat, inv, scaled):
    return inv * (
        scaled
        - jnp.mean(scaled, axis=-1, keepdims=True)
        - xhat * jnp.mean(scaled * xhat, axis=-1, keepdims=True)
    )


def layer(
    clip_tokens,
    frame_counts,
    attn_qkv,
    attn_out,
    mlp_in,
    mlp_out,
    align_proj,
    norm_gains,
    layer_biases,
    hidden_bias,
    align_bias,
    out_cotangent,
    align_cotangent,
):
    n_dp = lax.axis_size("dp")
    me = lax.axis_index("dp")
    rank = lax.axis_index("tensor")
    first = rank == 0
    half = clip_tokens.shape[1]
    width = clip_tokens.shape[2]
    all_rows = 2 * half
    block = width // n_dp
    head_width = attn_qkv.shape[2]
    heads = head_width // HEAD_DIM
    hidden_width = mlp_in.shape[1]
    align_width = align_proj.shape[1]
    align_half = align_width // 2
    sub = align_proj.shape[0]
    score_scale = HEAD_DIM ** (-0.5)

    masks = jnp.array(block_masks(), dtype=jnp.int32)
    owners = me ^ masks
    feature = jnp.arange(width, dtype=jnp.int32)
    absolute = jnp.repeat(owners, block) * block + feature % block
    permute = (feature[:, None] == absolute[None, :]).astype(jnp.float32)

    small = jnp.concatenate(
        [norm_gains.reshape(-1), layer_biases.reshape(-1), hidden_bias, align_bias]
    )
    count = small.shape[0]
    near = gather_far(attn_qkv.reshape(block, 3 * head_width))
    small_far = swap(small)
    small_rel = jnp.where(
        first, jnp.concatenate([small, small_far]), jnp.concatenate([small_far, small])
    ).reshape(1, -1)
    for bit in inner_bits() + [2, 1, 0]:
        small_rel = jnp.concatenate([small_rel, exchange(small_rel, bit)])
    one_near_y, one_near_x = exchange(near, 1), exchange(near, 0)
    away = exchange(near, 2)
    one_away_y, one_away_x = exchange(away, 1), exchange(away, 0)
    one_near_xy = exchange(one_near_y, 0)
    one_away_xy = exchange(one_away_x, 1)
    qkv_all = jnp.concatenate(
        [near, away, one_near_y, one_away_x, one_near_xy, one_near_x, one_away_xy, one_away_y]
    )

    align_other = swap(align_proj)
    align_rows = jnp.where(
        first,
        jnp.concatenate([align_proj[:, :align_half], align_other[:, :align_half]]),
        jnp.concatenate([align_other[:, align_half:], align_proj[:, align_half:]]),
    )
    two_shard = jnp.concatenate([attn_out.T, align_rows], axis=1)
    two_near = gather_far(after(two_shard, away))
    two_quarter = jnp.concatenate([two_near, exchange(two_near, 2)])
    three_near = gather_far(after(mlp_in, two_near))

    natural = inner_bits() + [2, 1, 0]
    bits = [sum((j >> i & 1) << bit for i, bit in enumerate(natural)) for j in range(n_dp)]
    from_me = me ^ jnp.array(bits, dtype=jnp.int32)
    small_hot = (jnp.arange(n_dp, dtype=jnp.int32)[:, None] == from_me[None, :]).astype(jnp.float32)
    small_abs = mm(small_hot, small_rel, HIGHEST)
    small_abs = small_abs.reshape(n_dp, 2, count)
    gains = small_abs[:, :, : 2 * sub].reshape(n_dp, 2, 2, sub)
    gains = jnp.transpose(gains, (2, 0, 1, 3)).reshape(2, width)
    biases = small_abs[:, :, 2 * sub : 8 * sub].reshape(n_dp, 2, 6, sub)
    biases = jnp.transpose(biases, (2, 0, 1, 3)).reshape(6, width)
    hidden_at = 8 * sub
    align_at = hidden_at + hidden_bias.shape[0]
    hidden_all = small_abs[:, :, hidden_at:align_at].reshape(-1)
    align_shift = small_abs[:, :, align_at:].reshape(-1)
    vectors = mm(jnp.concatenate([gains, biases]), permute, HIGHEST)
    gain_one, gain_two, shift_one, shift_two = vectors[0], vectors[1], vectors[2], vectors[3]
    shift_out, shift_down = vectors[6], vectors[7]
    query_shift = jnp.where(first, biases[2, :head_width], biases[2, head_width:])
    value_shift = jnp.where(first, biases[3, :head_width], biases[3, head_width:])
    hidden_shift = jnp.where(first, hidden_all[:hidden_width], hidden_all[hidden_width:])

    kept = (frame_counts[0] * FULL_TOK + 15) // 16
    position = jnp.arange(half, dtype=jnp.int32)
    index = jnp.concatenate([rank * half + position, (1 - rank) * half + position])
    valid = index < kept
    row_mask = valid[:half].astype(jnp.float32)[:, None]

    def both(terms):
        got = swap(terms)
        return terms + jnp.concatenate([got[half:], got[:half]])

    tokens = mm(clip_tokens[0], permute, HIGHEST)
    tokens = jnp.concatenate([tokens, swap(tokens)])
    cotangent = mm(out_cotangent[0], permute, HIGHEST)
    xhat_one, inv_one = centre(tokens)

    normed_one = xhat_one * gain_one + shift_one
    two_sides = gather_side(after(two_quarter, one_near_xy, one_away_xy))
    mixed = mm(normed_one, qkv_all)
    query = (mixed[:, :head_width] + query_shift).reshape(all_rows, heads, HEAD_DIM)
    key = mixed[:, head_width : 2 * head_width].reshape(all_rows, heads, HEAD_DIM)
    value = (mixed[:, 2 * head_width :] + value_shift).reshape(all_rows, heads, HEAD_DIM)
    three_quarter = jnp.concatenate([three_near, exchange(three_near, 2)])
    two_corners = gather_corner(two_sides)
    scores = heads_mm("qhe,khe->hqk", query, key) * score_scale
    scores = jnp.where(valid[None, None, :], scores, NEG_FILL)
    maxima = jnp.max(scores, axis=2, keepdims=True)
    expon = jnp.exp(scores - maxima)
    totals = jnp.sum(expon, axis=2, keepdims=True)
    probs = expon / totals
    heads_out = heads_mm("hqk,khe->qhe", probs, value).reshape(all_rows, head_width)
    two_all = assemble(two_quarter, two_sides, two_corners)
    out_all, align_mine = two_all[:, :head_width], two_all[:, head_width:]
    three_sides = gather_side(three_quarter)
    four_near = gather_far(after(mlp_out.T, three_quarter))
    attn_terms = mm_nt(heads_out, out_all)
    residual = tokens + both(attn_terms) + shift_out

    align_far = swap(align_mine)
    align_all = jnp.where(
        first,
        jnp.concatenate([align_mine, align_far], axis=1),
        jnp.concatenate([align_far, align_mine], axis=1),
    )
    align_grad = row_mask * align_cotangent[0]
    own_grad = row_mask * (cotangent + mm_nt(align_grad, align_all))
    own_sum = jnp.sum(own_grad, axis=0)
    out_grad = jnp.concatenate([own_grad, swap(own_grad)])

    four_quarter = jnp.concatenate([four_near, exchange(four_near, 2)])
    three_corners = gather_corner(three_sides)
    in_all = assemble(three_quarter, three_sides, three_corners)
    four_sides = gather_side(after(four_quarter, three_corners[0], three_corners[1]))
    four_corners = gather_corner(four_sides)
    down_all = assemble(four_quarter, four_sides, four_corners)
    xhat_two, inv_two = centre(residual)
    normed_two = xhat_two * gain_two + shift_two
    middle = width // 2
    pre_act = mm(normed_two, in_all) + hidden_shift
    normal_cdf = 0.5 * (1.0 + lax.erf(pre_act * INV_ROOT_TWO))
    activ = pre_act * normal_cdf
    slope = normal_cdf + pre_act * (jnp.exp(-0.5 * pre_act * pre_act) * INV_ROOT_TWO_PI)
    down_sent = mm_tn(out_grad[:, middle:], activ)
    down_rest = mm_tn(out_grad[:, :middle], activ)
    down_got = reduce_send(after(down_sent, four_corners[0], four_corners[1]))
    down_turned = reduce_turn(down_rest, down_got)
    grad_down_own = reduce_far(reduce_near(down_rest, down_got, down_turned))
    grad_act = mm(out_grad, down_all) * slope
    hidden_sum = jnp.sum(grad_act, axis=0)
    grad_normed_two = both(mm_nt(grad_act, in_all))
    in_sent = mm_tn(normed_two[:, middle:], grad_act)
    in_rest = mm_tn(normed_two[:, :middle], grad_act)
    in_got = reduce_send(in_sent)
    in_turned = reduce_turn(in_rest, in_got)
    grad_in_own = reduce_far(reduce_near(in_rest, in_got, in_turned))

    mlp_terms = mm_nt(activ, down_all)
    mlp_local = mlp_terms[:half] + swap(mlp_terms[half:])
    block_rel = row_mask * (residual[:half] + mlp_local + shift_down)
    grad_align = mm_tn(block_rel, align_grad)
    align_left, align_right = grad_align[:, :align_half], grad_align[:, align_half:]
    grad_align_half = jnp.where(first, align_left, align_right) + swap(
        jnp.where(first, align_right, align_left)
    )

    grad_residual = out_grad + norm_back(xhat_two, inv_two, grad_normed_two * gain_two)
    heads_grad = mm(grad_residual, out_all)
    grad_out = mm_tn(grad_residual, heads_out)
    grad_two = jnp.concatenate([grad_out, grad_align_half], axis=1)
    two_got = reduce_send(grad_two[middle:])
    two_turned = reduce_turn(grad_two[:middle], two_got)
    two_own = reduce_far(reduce_near(grad_two[:middle], two_got, two_turned))

    grad_split = heads_grad.reshape(all_rows, heads, HEAD_DIM)
    out_split = heads_out.reshape(all_rows, heads, HEAD_DIM)
    value_grad = heads_mm("hqk,qhe->khe", probs, grad_split).reshape(all_rows, head_width)
    value_part = jnp.sum(value_grad, axis=0)
    row_dot = jnp.transpose(jnp.sum(grad_split * out_split, axis=2))[:, :, None]
    probs_grad = heads_mm("qhe,khe->hqk", grad_split, value)
    score_grad = probs * (probs_grad - row_dot) * score_scale
    query_grad = heads_mm("hqk,khe->qhe", score_grad, key).reshape(all_rows, head_width)
    query_part = jnp.sum(query_grad, axis=0)
    key_grad = heads_mm("hqk,qhe->khe", score_grad, query).reshape(all_rows, head_width)
    mixed_grad = jnp.concatenate([query_grad, key_grad, value_grad], axis=1)
    one_upper = mm_tn(normed_one[:, middle:], mixed_grad)
    one_lower = mm_tn(normed_one[:, :middle], mixed_grad)
    one_got = reduce_send(one_upper)
    one_turned = reduce_turn(one_lower, one_got)
    grad_qkv_own = reduce_far(reduce_near(one_lower, one_got, one_turned))
    one_terms = mm_nt(mixed_grad, qkv_all)
    grad_normed_one = one_terms[:half] + swap(one_terms[half:])
    xhat_own, inv_own = xhat_one[:half], inv_one[:half]
    tokens_rel = grad_residual[:half] + norm_back(xhat_own, inv_own, grad_normed_one * gain_one)
    align_out = row_mask * (mm(block_rel, align_all) + align_shift)
    back = mm_nt(jnp.concatenate([block_rel, tokens_rel]), permute, HIGHEST)
    block_out, grad_tokens = back[:half], back[half:]
    grad_out_own, grad_align_pair = two_own[:, :head_width], two_own[:, head_width:]

    norm_own = grad_normed_two[:half]
    relative = jnp.stack(
        [
            jnp.sum(grad_normed_one * xhat_own, axis=0),
            jnp.sum(norm_own * xhat_two[:half], axis=0),
            jnp.sum(grad_normed_one, axis=0),
            jnp.sum(norm_own, axis=0),
            jnp.sum(grad_residual[:half], axis=0),
            own_sum,
        ]
    )
    vectors = mm_nt(relative, permute, HIGHEST)

    def placed_half(part):
        zero = jnp.zeros_like(part)
        return jnp.where(first, jnp.concatenate([part, zero]), jnp.concatenate([zero, part]))

    query_part, value_part, hidden_sum = lax.optimization_barrier(
        (query_part, value_part, hidden_sum, one_lower)
    )[:3]
    query_sum = placed_half(query_part)
    value_sum = placed_half(value_part)
    rows = jnp.concatenate(
        [vectors[:4], query_sum[None], value_sum[None], vectors[4:]]
    )
    rows = jnp.transpose(rows.reshape(8, n_dp, 2, sub), (1, 2, 0, 3)).reshape(n_dp, 2, 8 * sub)
    hidden_rows = placed_half(hidden_sum).reshape(n_dp, 2, -1)
    align_rows_sum = jnp.sum(align_grad, axis=0).reshape(n_dp, 2, -1)
    packed = jnp.concatenate([rows, hidden_rows, align_rows_sum], axis=2)
    packed_own = jnp.where(first, packed[:, 0], packed[:, 1]) + swap(
        jnp.where(first, packed[:, 1], packed[:, 0])
    )
    reduced = mm_tn(small_hot, packed_own, HIGHEST)
    for bit in reversed(natural):
        size = reduced.shape[0] // 2
        reduced = reduced[:size] + exchange(reduced[size:], bit)
    reduced = reduced[0]

    mine = jnp.where(first, grad_align_pair[:sub], grad_align_pair[sub:])
    others = swap(jnp.where(first, grad_align_pair[sub:], grad_align_pair[:sub]))
    align_own = jnp.where(
        first,
        jnp.concatenate([mine, others], axis=1),
        jnp.concatenate([others, mine], axis=1),
    )
    return (
        block_out[None],
        align_out[None],
        grad_tokens[None],
        grad_qkv_own.reshape(block, 3, head_width),
        grad_out_own.T,
        grad_in_own,
        grad_down_own.T,
        align_own,
        reduced[: 2 * sub].reshape(2, sub),
        reduced[2 * sub : 8 * sub].reshape(6, sub),
        reduced[hidden_at:align_at],
        reduced[align_at:],
    )


def solution(mesh):
    placed = (
        P("dp", "tensor", None),
        P("dp"),
        P("dp", None, "tensor"),
        P("tensor", "dp"),
        P("dp", "tensor"),
        P("tensor", "dp"),
        P(("dp", "tensor"), None),
        P(None, ("dp", "tensor")),
        P(None, ("dp", "tensor")),
        P(("dp", "tensor")),
        P(("dp", "tensor")),
        P("dp", "tensor", None),
        P("dp", "tensor", None),
    )
    return jax.shard_map(
        layer,
        mesh=mesh,
        in_specs=placed,
        out_specs=(
            P("dp", "tensor", None),
            P("dp", "tensor", None),
            P("dp", "tensor", None),
            P("dp", None, "tensor"),
            P("tensor", "dp"),
            P("dp", "tensor"),
            P("tensor", "dp"),
            P(("dp", "tensor"), None),
            P(None, ("dp", "tensor")),
            P(None, ("dp", "tensor")),
            P(("dp", "tensor")),
            P(("dp", "tensor")),
        ),
        check_vma=False,
    )
```

```python
import math

import jax
import jax.numpy as jnp
from jax import lax
from jax.sharding import PartitionSpec as P

HEAD_DIM = 64
FULL_TOK = 627

HIGH = lax.Precision.HIGH
HIGHEST = lax.Precision.HIGHEST
EPSILON = 1e-06
NEG_FILL = -1e30
INV_ROOT_TWO = 1.0 / math.sqrt(2.0)
INV_ROOT_TWO_PI = 1.0 / math.sqrt(2.0 * math.pi)


def product(left, right, left_dim, right_dim, precision=HIGH):
    return lax.dot_general(
        left,
        right,
        (((left_dim,), (right_dim,)), ((), ())),
        precision=precision,
        preferred_element_type=jnp.float32,
    )


def mm(left, right, precision=HIGH):
    return product(left, right, 1, 0, precision)


def mm_nt(left, right, precision=HIGH):
    return product(left, right, 1, 1, precision)


def mm_tn(left, right, precision=HIGH):
    return product(left, right, 0, 0, precision)


def heads_mm(form, left, right):
    return jnp.einsum(form, left, right, precision=HIGH, preferred_element_type=jnp.float32)


def swap(values):
    return lax.ppermute(values, "tensor", [(0, 1), (1, 0)])


def exchange(values, bit):
    n_dp = lax.axis_size("dp")
    return lax.ppermute(values, "dp", [(i, i ^ (1 << bit)) for i in range(n_dp)])


def after(value, *others):
    return lax.optimization_barrier((value, *others))[0]


def inner_bits():
    return list(range(3, (lax.axis_size("dp") - 1).bit_length()))


EIGHTHS = (0, 1, 2, 5, 6, 4, 7, 3)


def block_masks():
    n_dp = lax.axis_size("dp")
    inner = inner_bits()
    masks = []
    for eighth in EIGHTHS:
        outer = (eighth >> 2 & 1) | (eighth >> 1 & 1) << 1 | (eighth & 1) << 2
        for j in range(n_dp // 8):
            masks.append(outer | sum((j >> i & 1) << bit for i, bit in enumerate(inner)))
    return masks


def gather_far(shard):
    near = shard
    for bit in inner_bits():
        near = jnp.concatenate([near, exchange(near, bit)])
    return near


def gather_side(quarter):
    return exchange(quarter, 1), exchange(quarter, 0)


def gather_corner(sides):
    side_y, side_x = sides
    eighth = side_y.shape[0] // 2
    low, high = lax.optimization_barrier((side_y[:eighth], side_x[eighth:]))
    return exchange(low, 0), exchange(high, 1)


def assemble(quarter, sides, corners):
    side_y, side_x = sides
    eighth = side_y.shape[0] // 2
    return jnp.concatenate(
        [
            quarter,
            side_y[:eighth],
            side_x[eighth:],
            corners[0],
            side_x[:eighth],
            corners[1],
            side_y[eighth:],
        ]
    )


def reduce_send(upper):
    quarter = upper.shape[0] // 2
    return exchange(upper[:quarter], 0), exchange(upper[quarter:], 1)


def reduce_turn(lower, got):
    eighth = lower.shape[0] // 4
    got_x, got_y = got
    by_y = exchange(lower[2 * eighth : 3 * eighth] + got_x[:eighth], 1)
    by_x = exchange(lower[3 * eighth :] + got_y[:eighth], 0)
    return by_y, by_x


def reduce_near(lower, got, turned):
    eighth = lower.shape[0] // 4
    got_x, got_y = got
    by_y, by_x = turned
    away = exchange(lower[eighth : 2 * eighth] + got_y[eighth:] + by_x, 2)
    return lower[:eighth] + got_x[eighth:] + by_y + away


def reduce_far(total):
    for bit in reversed(inner_bits()):
        count = total.shape[0] // 2
        total = total[:count] + exchange(total[count:], bit)
    return total


def centre(values):
    row_mean = jnp.mean(values, axis=-1, keepdims=True)
    centred = values - row_mean
    variance = jnp.mean(centred * centred, axis=-1, keepdims=True)
    inv = lax.rsqrt(variance + EPSILON)
    return centred * inv, inv


def norm_back(xhat, inv, scaled):
    return inv * (
        scaled
        - jnp.mean(scaled, axis=-1, keepdims=True)
        - xhat * jnp.mean(scaled * xhat, axis=-1, keepdims=True)
    )


def layer(
    clip_tokens,
    frame_counts,
    attn_qkv,
    attn_out,
    mlp_in,
    mlp_out,
    align_proj,
    norm_gains,
    layer_biases,
    hidden_bias,
    align_bias,
    out_cotangent,
    align_cotangent,
):
    n_dp = lax.axis_size("dp")
    me = lax.axis_index("dp")
    rank = lax.axis_index("tensor")
    first = rank == 0
    half = clip_tokens.shape[1]
    width = clip_tokens.shape[2]
    all_rows = 2 * half
    block = width // n_dp
    head_width = attn_qkv.shape[2]
    heads = head_width // HEAD_DIM
    hidden_width = mlp_in.shape[1]
    align_width = align_proj.shape[1]
    align_half = align_width // 2
    sub = align_proj.shape[0]
    score_scale = HEAD_DIM ** (-0.5)

    masks = jnp.array(block_masks(), dtype=jnp.int32)
    owners = me ^ masks
    feature = jnp.arange(width, dtype=jnp.int32)
    absolute = jnp.repeat(owners, block) * block + feature % block
    permute = (feature[:, None] == absolute[None, :]).astype(jnp.float32)

    small = jnp.concatenate(
        [norm_gains.reshape(-1), layer_biases.reshape(-1), hidden_bias, align_bias]
    )
    count = small.shape[0]
    near = gather_far(attn_qkv.reshape(block, 3 * head_width))
    small_far = swap(small)
    small_rel = jnp.where(
        first, jnp.concatenate([small, small_far]), jnp.concatenate([small_far, small])
    ).reshape(1, -1)
    for bit in inner_bits() + [2, 1, 0]:
        small_rel = jnp.concatenate([small_rel, exchange(small_rel, bit)])
    one_near_y, one_near_x = exchange(near, 1), exchange(near, 0)
    away = exchange(near, 2)
    one_away_y, one_away_x = exchange(away, 1), exchange(away, 0)
    one_near_xy = exchange(one_near_y, 0)
    one_away_xy = exchange(one_away_x, 1)
    qkv_all = jnp.concatenate(
        [near, away, one_near_y, one_away_x, one_near_xy, one_near_x, one_away_xy, one_away_y]
    )

    align_other = swap(align_proj)
    align_rows = jnp.where(
        first,
        jnp.concatenate([align_proj[:, :align_half], align_other[:, :align_half]]),
        jnp.concatenate([align_other[:, align_half:], align_proj[:, align_half:]]),
    )
    two_shard = jnp.concatenate([attn_out.T, align_rows], axis=1)
    two_near = gather_far(after(two_shard, away))
    two_quarter = jnp.concatenate([two_near, exchange(two_near, 2)])
    three_near = gather_far(after(mlp_in, two_near))

    natural = inner_bits() + [2, 1, 0]
    bits = [sum((j >> i & 1) << bit for i, bit in enumerate(natural)) for j in range(n_dp)]
    from_me = me ^ jnp.array(bits, dtype=jnp.int32)
    small_hot = (jnp.arange(n_dp, dtype=jnp.int32)[:, None] == from_me[None, :]).astype(jnp.float32)
    small_abs = mm(small_hot, small_rel, HIGHEST)
    small_abs = small_abs.reshape(n_dp, 2, count)
    gains = small_abs[:, :, : 2 * sub].reshape(n_dp, 2, 2, sub)
    gains = jnp.transpose(gains, (2, 0, 1, 3)).reshape(2, width)
    biases = small_abs[:, :, 2 * sub : 8 * sub].reshape(n_dp, 2, 6, sub)
    biases = jnp.transpose(biases, (2, 0, 1, 3)).reshape(6, width)
    hidden_at = 8 * sub
    align_at = hidden_at + hidden_bias.shape[0]
    hidden_all = small_abs[:, :, hidden_at:align_at].reshape(-1)
    align_shift = small_abs[:, :, align_at:].reshape(-1)
    vectors = mm(jnp.concatenate([gains, biases]), permute, HIGHEST)
    gain_one, gain_two, shift_one, shift_two = vectors[0], vectors[1], vectors[2], vectors[3]
    shift_out, shift_down = vectors[6], vectors[7]
    query_shift = jnp.where(first, biases[2, :head_width], biases[2, head_width:])
    value_shift = jnp.where(first, biases[3, :head_width], biases[3, head_width:])
    hidden_shift = jnp.where(first, hidden_all[:hidden_width], hidden_all[hidden_width:])

    kept = (frame_counts[0] * FULL_TOK + 15) // 16
    position = jnp.arange(half, dtype=jnp.int32)
    index = jnp.concatenate([rank * half + position, (1 - rank) * half + position])
    valid = index < kept
    row_mask = valid[:half].astype(jnp.float32)[:, None]

    def both(terms):
        got = swap(terms)
        return terms + jnp.concatenate([got[half:], got[:half]])

    tokens = mm(clip_tokens[0], permute)
    tokens = jnp.concatenate([tokens, swap(tokens)])
    cotangent = mm(out_cotangent[0], permute)
    xhat_one, inv_one = centre(tokens)

    normed_one = xhat_one * gain_one + shift_one
    two_sides = gather_side(after(two_quarter, one_near_xy, one_away_xy))
    mixed = mm(normed_one, qkv_all)
    query = (mixed[:, :head_width] + query_shift).reshape(all_rows, heads, HEAD_DIM)
    key = mixed[:, head_width : 2 * head_width].reshape(all_rows, heads, HEAD_DIM)
    value = (mixed[:, 2 * head_width :] + value_shift).reshape(all_rows, heads, HEAD_DIM)
    three_quarter = jnp.concatenate([three_near, exchange(three_near, 2)])
    two_corners = gather_corner(two_sides)
    scores = heads_mm("qhe,khe->hqk", query, key) * score_scale
    scores = jnp.where(valid[None, None, :], scores, NEG_FILL)
    maxima = jnp.max(scores, axis=2, keepdims=True)
    expon = jnp.exp(scores - maxima)
    totals = jnp.sum(expon, axis=2, keepdims=True)
    probs = expon / totals
    heads_out = heads_mm("hqk,khe->qhe", probs, value).reshape(all_rows, head_width)
    two_all = assemble(two_quarter, two_sides, two_corners)
    out_all, align_mine = two_all[:, :head_width], two_all[:, head_width:]
    three_sides = gather_side(three_quarter)
    four_near = gather_far(after(mlp_out.T, three_quarter))
    attn_terms = mm_nt(heads_out, out_all)
    residual = tokens + both(attn_terms) + shift_out

    align_far = swap(align_mine)
    align_all = jnp.where(
        first,
        jnp.concatenate([align_mine, align_far], axis=1),
        jnp.concatenate([align_far, align_mine], axis=1),
    )
    align_grad = row_mask * align_cotangent[0]
    own_grad = row_mask * (cotangent + mm_nt(align_grad, align_all))
    own_sum = jnp.sum(own_grad, axis=0)
    out_grad = jnp.concatenate([own_grad, swap(own_grad)])

    four_quarter = jnp.concatenate([four_near, exchange(four_near, 2)])
    three_corners = gather_corner(three_sides)
    in_all = assemble(three_quarter, three_sides, three_corners)
    four_sides = gather_side(after(four_quarter, three_corners[0], three_corners[1]))
    four_corners = gather_corner(four_sides)
    down_all = assemble(four_quarter, four_sides, four_corners)
    xhat_two, inv_two = centre(residual)
    normed_two = xhat_two * gain_two + shift_two
    middle = width // 2
    pre_act = mm(normed_two, in_all) + hidden_shift
    normal_cdf = 0.5 * (1.0 + lax.erf(pre_act * INV_ROOT_TWO))
    activ = pre_act * normal_cdf
    slope = normal_cdf + pre_act * (jnp.exp(-0.5 * pre_act * pre_act) * INV_ROOT_TWO_PI)
    down_sent = mm_tn(out_grad[:, middle:], activ)
    down_rest = mm_tn(out_grad[:, :middle], activ)
    down_got = reduce_send(after(down_sent, four_corners[0], four_corners[1]))
    down_turned = reduce_turn(down_rest, down_got)
    grad_down_own = reduce_far(reduce_near(down_rest, down_got, down_turned))
    grad_act = mm(out_grad, down_all) * slope
    hidden_sum = jnp.sum(grad_act, axis=0)
    grad_normed_two = both(mm_nt(grad_act, in_all))
    in_sent = mm_tn(normed_two[:, middle:], grad_act)
    in_rest = mm_tn(normed_two[:, :middle], grad_act)
    in_got = reduce_send(in_sent)
    in_turned = reduce_turn(in_rest, in_got)
    grad_in_own = reduce_far(reduce_near(in_rest, in_got, in_turned))

    mlp_terms = mm_nt(activ, down_all)
    mlp_local = mlp_terms[:half] + swap(mlp_terms[half:])
    block_rel = row_mask * (residual[:half] + mlp_local + shift_down)
    grad_align = mm_tn(block_rel, align_grad)
    align_left, align_right = grad_align[:, :align_half], grad_align[:, align_half:]
    grad_align_half = jnp.where(first, align_left, align_right) + swap(
        jnp.where(first, align_right, align_left)
    )

    grad_residual = out_grad + norm_back(xhat_two, inv_two, grad_normed_two * gain_two)
    heads_grad = mm(grad_residual, out_all)
    grad_out = mm_tn(grad_residual, heads_out)
    grad_two = jnp.concatenate([grad_out, grad_align_half], axis=1)
    two_got = reduce_send(grad_two[middle:])
    two_turned = reduce_turn(grad_two[:middle], two_got)
    two_own = reduce_far(reduce_near(grad_two[:middle], two_got, two_turned))

    grad_split = heads_grad.reshape(all_rows, heads, HEAD_DIM)
    out_split = heads_out.reshape(all_rows, heads, HEAD_DIM)
    value_grad = heads_mm("hqk,qhe->khe", probs, grad_split).reshape(all_rows, head_width)
    value_part = jnp.sum(value_grad, axis=0)
    row_dot = jnp.transpose(jnp.sum(grad_split * out_split, axis=2))[:, :, None]
    probs_grad = heads_mm("qhe,khe->hqk", grad_split, value)
    score_grad = probs * (probs_grad - row_dot) * score_scale
    query_grad = heads_mm("hqk,khe->qhe", score_grad, key).reshape(all_rows, head_width)
    query_part = jnp.sum(query_grad, axis=0)
    key_grad = heads_mm("hqk,qhe->khe", score_grad, query).reshape(all_rows, head_width)
    mixed_grad = jnp.concatenate([query_grad, key_grad, value_grad], axis=1)
    one_upper = mm_tn(normed_one[:, middle:], mixed_grad)
    one_lower = mm_tn(normed_one[:, :middle], mixed_grad)
    one_got = reduce_send(one_upper)
    one_turned = reduce_turn(one_lower, one_got)
    grad_qkv_own = reduce_far(reduce_near(one_lower, one_got, one_turned))
    one_terms = mm_nt(mixed_grad, qkv_all)
    grad_normed_one = one_terms[:half] + swap(one_terms[half:])
    xhat_own, inv_own = xhat_one[:half], inv_one[:half]
    tokens_rel = grad_residual[:half] + norm_back(xhat_own, inv_own, grad_normed_one * gain_one)
    align_out = row_mask * (mm(block_rel, align_all) + align_shift)
    back = mm_nt(jnp.concatenate([block_rel, tokens_rel]), permute)
    block_out, grad_tokens = back[:half], back[half:]
    grad_out_own, grad_align_pair = two_own[:, :head_width], two_own[:, head_width:]

    norm_own = grad_normed_two[:half]
    relative = jnp.stack(
        [
            jnp.sum(grad_normed_one * xhat_own, axis=0),
            jnp.sum(norm_own * xhat_two[:half], axis=0),
            jnp.sum(grad_normed_one, axis=0),
            jnp.sum(norm_own, axis=0),
            jnp.sum(grad_residual[:half], axis=0),
            own_sum,
        ]
    )
    vectors = mm_nt(relative, permute, HIGHEST)

    def placed_half(part):
        zero = jnp.zeros_like(part)
        return jnp.where(first, jnp.concatenate([part, zero]), jnp.concatenate([zero, part]))

    query_part, value_part, hidden_sum = lax.optimization_barrier(
        (query_part, value_part, hidden_sum, one_lower)
    )[:3]
    query_sum = placed_half(query_part)
    value_sum = placed_half(value_part)
    rows = jnp.concatenate(
        [vectors[:4], query_sum[None], value_sum[None], vectors[4:]]
    )
    rows = jnp.transpose(rows.reshape(8, n_dp, 2, sub), (1, 2, 0, 3)).reshape(n_dp, 2, 8 * sub)
    hidden_rows = placed_half(hidden_sum).reshape(n_dp, 2, -1)
    align_rows_sum = jnp.sum(align_grad, axis=0).reshape(n_dp, 2, -1)
    packed = jnp.concatenate([rows, hidden_rows, align_rows_sum], axis=2)
    packed_own = jnp.where(first, packed[:, 0], packed[:, 1]) + swap(
        jnp.where(first, packed[:, 1], packed[:, 0])
    )
    reduced = mm_tn(small_hot, packed_own, HIGHEST)
    for bit in reversed(natural):
        size = reduced.shape[0] // 2
        reduced = reduced[:size] + exchange(reduced[size:], bit)
    reduced = reduced[0]

    mine = jnp.where(first, grad_align_pair[:sub], grad_align_pair[sub:])
    others = swap(jnp.where(first, grad_align_pair[sub:], grad_align_pair[:sub]))
    align_own = jnp.where(
        first,
        jnp.concatenate([mine, others], axis=1),
        jnp.concatenate([others, mine], axis=1),
    )
    return (
        block_out[None],
        align_out[None],
        grad_tokens[None],
        grad_qkv_own.reshape(block, 3, head_width),
        grad_out_own.T,
        grad_in_own,
        grad_down_own.T,
        align_own,
        reduced[: 2 * sub].reshape(2, sub),
        reduced[2 * sub : 8 * sub].reshape(6, sub),
        reduced[hidden_at:align_at],
        reduced[align_at:],
    )


def solution(mesh):
    placed = (
        P("dp", "tensor", None),
        P("dp"),
        P("dp", None, "tensor"),
        P("tensor", "dp"),
        P("dp", "tensor"),
        P("tensor", "dp"),
        P(("dp", "tensor"), None),
        P(None, ("dp", "tensor")),
        P(None, ("dp", "tensor")),
        P(("dp", "tensor")),
        P(("dp", "tensor")),
        P("dp", "tensor", None),
        P("dp", "tensor", None),
    )
    return jax.shard_map(
        layer,
        mesh=mesh,
        in_specs=placed,
        out_specs=(
            P("dp", "tensor", None),
            P("dp", "tensor", None),
            P("dp", "tensor", None),
            P("dp", None, "tensor"),
            P("tensor", "dp"),
            P("dp", "tensor"),
            P("tensor", "dp"),
            P(("dp", "tensor"), None),
            P(None, ("dp", "tensor")),
            P(None, ("dp", "tensor")),
            P(("dp", "tensor")),
            P(("dp", "tensor")),
        ),
        check_vma=False,
    )
```
